32 devices in a mesh: stream: 8 (over z, x), wall: 4 (over y, core).
Axes of the slice: x: 2, y: 2, z: 4, core: 2. Of those that a mesh axis runs over, the one named last changes fastest.
Arguments:
- source_grad: float32 [6, 128, 64, 128], P(None, 'stream', 'wall'), may hold values from -0.3 to 0.3
- wall_pivot: bfloat16 [6, 6, 128, 64, 128], P(None, None, 'stream', 'wall')
- wall_low: bfloat16 [6, 128, 64, 128], P(None, 'stream', 'wall')
- wall_up: bfloat16 [6, 128, 64, 128], P(None, 'stream', 'wall')
- stream_inverse: bfloat16 [6, 6, 128, 64, 128], P(None, None, 'stream', 'wall')
- stream_flux: bfloat16 [6, 128, 64, 128], P(None, 'stream', 'wall')
- remainder: bfloat16 [3, 6, 128, 64, 128], P(None, None, 'stream', 'wall')
- active_count: int32 [8, 64], P('stream', 'wall'), may hold values from 1 to 16, as said below
- cell_offset: int32 [8, 64], P('stream', 'wall'), may hold values from 0 to 15
Outputs:
- adjoint: float32 [6, 128, 64, 128], P(None, 'stream', 'wall')
The draws below stay inside these ranges and needn't reach their ends.
Inputs may be any that keep to these rules, and one draw needn't show every extreme that they name: active_count[b, j] + cell_offset[b, j] <= 16 for every entry.
All inputs are finite; a program needn't handle non-finite values.
Results may differ from the reference program's by a relative error of at most 0.0003.
Values sent between devices are 32-bit elements; how exact they have to be, the bound alone decides.
A program may use at most 128 MiB of HBM per device.

```python
import math
import jax
import jax.numpy as jnp
from jax import lax

NF = 6
CI = 16
CK = 128
ITERS = 2
NI = 128
NJ = 64
STREAM_BLOCKS = 8


def block_field(key, minimum_logarithm, high_log, spread):
    first_key, second_key = jax.random.split(key)
    full_shape = (NF, NF, NI, NJ, CK)
    offdiag = jnp.clip(jax.random.normal(first_key, full_shape, jnp.float32), -4.0, 4.0) * spread
    diagonal = jnp.exp(jax.random.uniform(second_key, (NF, NI, NJ, CK), jnp.float32, minimum_logarithm, high_log))
    unit_block = jnp.eye(NF, dtype=jnp.float32).reshape(NF, NF, 1, 1, 1)
    return ((1.0 - unit_block) * offdiag + unit_block * diagonal[None]).astype(jnp.bfloat16)


def rate_field(key, joined_chain_order, array_axis):
    stochastic_derived_seeds = jax.random.split(key, 5)
    full_shape = (NF, NI, NJ, CK)
    slow_count = 3
    ranking = jax.random.permutation(stochastic_derived_seeds[0], NF)
    slow_mask = (ranking < slow_count).reshape(NF, 1, 1, 1)
    slow_rates = jnp.exp(-jax.random.uniform(stochastic_derived_seeds[1], full_shape, jnp.float32, 0.5, 1.2) / joined_chain_order)
    fast_rates = jnp.exp(-jnp.exp(-jax.random.uniform(stochastic_derived_seeds[2], full_shape, jnp.float32, math.log(4.0), math.log(12.0))))
    rates = jnp.where(slow_mask, slow_rates, fast_rates)
    outbreak_opening_site = jax.random.randint(stochastic_derived_seeds[3], (3,), 0, joined_chain_order)
    outbreak_extent = jax.random.uniform(stochastic_derived_seeds[4], (3,), jnp.float32, 0.65, 0.85)
    grid_location = jnp.arange(joined_chain_order)
    scaling_factor = jnp.prod(jnp.where(grid_location[:, None] == outbreak_opening_site[None], outbreak_extent[None], 1.0), axis=1)
    layout_shape = [1, 1, 1, 1]
    layout_shape[array_axis] = joined_chain_order
    return (rates * scaling_factor.reshape(layout_shape)).astype(jnp.bfloat16)


def zone_layout(key):
    stochastic_derived_seeds = jax.random.split(jax.random.fold_in(key, 41), 4)
    entries = STREAM_BLOCKS * NJ
    counts = jax.random.randint(stochastic_derived_seeds[0], (entries,), 1, CI + 1)
    full_at = jax.random.randint(stochastic_derived_seeds[1], (), 0, entries)
    single_at = (full_at + jax.random.randint(stochastic_derived_seeds[2], (), 1, entries)) % entries
    counts = counts.at[full_at].set(CI).at[single_at].set(1)
    offsets = jax.random.randint(stochastic_derived_seeds[3], (entries,), 0, CI - counts + 1)
    offsets = offsets.at[single_at].set(CI - 1)
    return (counts.reshape(STREAM_BLOCKS, NJ), offsets.reshape(STREAM_BLOCKS, NJ))


def draw_wall_pivot(key, part):
    return block_field(jax.random.fold_in(key, 21), math.log(0.95), math.log(1.01), 0.09)


def draw_stream_inverse(key, part):
    return block_field(jax.random.fold_in(key, 22), math.log(0.95), math.log(1.01), 0.09)


def draw_wall_low(key, part):
    return rate_field(jax.random.fold_in(key, 11), NJ, 2)


def draw_wall_up(key, part):
    return rate_field(jax.random.fold_in(key, 12), NJ, 2)


def draw_stream_flux(key, part):
    return rate_field(jax.random.fold_in(key, 13), NI, 1)


def draw_remainder(key, part):
    subkey = jax.random.fold_in(key, 31)
    full_shape = (3, NF, NI, NJ, CK)
    scaling_factor = 0.4 / math.sqrt(NI * NJ)
    values = jnp.clip(jax.random.normal(subkey, full_shape, jnp.float32), -4.0, 4.0)
    return (values * scaling_factor).astype(jnp.bfloat16)


def draw_active_count(key, part):
    return zone_layout(key)[0]


def draw_cell_offset(key, part):
    return zone_layout(key)[1]


def levels(own_key, dims, cuts, smallest, top_value):
    factor_of = 1.0
    for dim, shards_of in cuts:
        draws = jax.random.uniform(jax.random.fold_in(jax.random.fold_in(own_key, 6), dim), (shards_of,), jnp.float32, smallest / len(cuts), top_value / len(cuts))
        factor_of = factor_of * jnp.repeat(jnp.exp(draws), dims[dim] // shards_of).reshape((-1,) + (1,) * (len(dims) - 1 - dim))
    return factor_of


def normal_values(rng, extent, deviation, limit, cuts=(), kind=jnp.bfloat16):
    values = deviation * jax.random.normal(rng, extent, jnp.float32)
    if cuts:
        values = values * levels(rng, extent, cuts, -0.22, 0.18)
    return jnp.clip(values, -limit, limit).astype(kind)


def setup_inputs(seed: int = 0) -> dict:
    keys = jax.random.split(jax.random.key(seed), 10)
    return {
        "source_grad": normal_values(keys[0], (NF, NI, NJ, CK), 0.05, 0.3, ((1, 8), (2, 4)), jnp.float32),
        "wall_pivot": draw_wall_pivot(jax.random.fold_in(keys[9], 71), 0),
        "wall_low": draw_wall_low(jax.random.fold_in(keys[9], 71), 0),
        "wall_up": draw_wall_up(jax.random.fold_in(keys[9], 71), 0),
        "stream_inverse": draw_stream_inverse(jax.random.fold_in(keys[9], 71), 0),
        "stream_flux": draw_stream_flux(jax.random.fold_in(keys[9], 71), 0),
        "remainder": draw_remainder(jax.random.fold_in(keys[9], 71), 0),
        "active_count": draw_active_count(jax.random.fold_in(keys[9], 71), 0),
        "cell_offset": draw_cell_offset(jax.random.fold_in(keys[9], 71), 0),
    }


def apply_block(block, vector):
    return jnp.sum(block.astype(jnp.float32) * vector[None], axis=1)


def apply_transposed(block, vector):
    return jnp.sum(block.astype(jnp.float32) * vector[:, None], axis=0)


def active_mask(active_count, cell_offset):
    grid_location = (jnp.arange(NI, dtype=jnp.int32) % CI)[:, None]
    counts = jnp.repeat(active_count, CI, axis=0)
    offsets = jnp.repeat(cell_offset, CI, axis=0)
    inside = (grid_location >= offsets) & (grid_location < offsets + counts)
    return jnp.where(inside, 1.0, 0.0).astype(jnp.float32)[None, :, :, None]


def smooth(source, wall_pivot, wall_low, wall_up, stream_inverse, stream_flux, enabled_flag):
    pivots = jnp.moveaxis(wall_pivot, 3, 0)
    lows = jnp.moveaxis(wall_low, 2, 0)
    highs = jnp.moveaxis(wall_up, 2, 0)
    sources = jnp.moveaxis(source, 2, 0)

    def lower_cell(carried, inputs):
        block, coupling, given = inputs
        updated = apply_block(block, given + coupling.astype(jnp.float32) * carried)
        return updated, updated

    line_zero = jnp.zeros((NF, NI, CK), jnp.float32)
    _, lower_pass = lax.scan(lower_cell, line_zero, (pivots, lows, sources))

    def upper_cell(carried, inputs):
        block, coupling, given = inputs
        updated = given + apply_block(block, coupling.astype(jnp.float32) * carried)
        return updated, updated

    _, upper_pass = lax.scan(upper_cell, line_zero, (pivots, highs, lower_pass), reverse=True)
    line_field = jnp.moveaxis(upper_pass, 0, 2)
    inverses = jnp.moveaxis(stream_inverse, 2, 0)
    fluxes = jnp.moveaxis(stream_flux, 1, 0)
    givens = jnp.moveaxis(line_field, 1, 0)
    actives = jnp.moveaxis(enabled_flag, 1, 0)

    def sweep_cell(carried, inputs):
        block, coupling, given, active_now = inputs
        updated = apply_transposed(block, given + coupling.astype(jnp.float32) * carried)
        updated = active_now * updated + (1.0 - active_now) * carried
        return updated, updated

    plane_zero = jnp.zeros((NF, NJ, CK), jnp.float32)
    _, swept = lax.scan(sweep_cell, plane_zero, (inverses, fluxes, givens, actives), reverse=True)
    return jnp.moveaxis(swept, 0, 1) * enabled_flag


def remainder_term(adjoint, remainder):
    padded = jnp.pad(adjoint, ((0, 0), (0, 1), (1, 1), (0, 0)))
    below_cells = padded[:, :-1, :-2]
    above_cells = padded[:, :-1, 2:]
    ahead_cells = padded[:, 1:, 1:-1]
    total = remainder[0].astype(jnp.float32) * below_cells
    total = total + remainder[1].astype(jnp.float32) * above_cells
    return total + remainder[2].astype(jnp.float32) * ahead_cells


def reference(source_grad, wall_pivot, wall_low, wall_up, stream_inverse, stream_flux, remainder, active_count, cell_offset):
    enabled_flag = active_mask(active_count, cell_offset)
    adjoint = jnp.zeros(source_grad.shape, jnp.float32)
    for sweep_round in range(ITERS):
        adjoint = smooth(source_grad + remainder_term(adjoint, remainder), wall_pivot, wall_low, wall_up, stream_inverse, stream_flux, enabled_flag)
    return adjoint
```

```python
import functools

import jax
import jax.numpy as jnp
from jax import lax
from jax.experimental import pallas as pl
from jax.experimental.pallas import tpu as pltpu
from jax.sharding import PartitionSpec as P

MESH = pl.DeviceIdType.MESH
ITERS = 2


def tree_sum(terms):
    while len(terms) > 1:
        paired = [terms[k] + terms[k + 1] for k in range(0, len(terms) - 1, 2)]
        if len(terms) % 2:
            paired.append(terms[-1])
        terms = paired
    return terms[0]


def kernel(
    ns, nw, NF, CI, CJ,
    src, wp, wl, wu, si, fl, rem, cnt, off,
    out,
    pt, rhs, low, up, lpt, upn, sif, flf,
    ss, oo, cin, cout, lin, lout, uin, uout,
    hlo_out, hhi_out, hlo, hhi, rlo, rhi, psi, mrow, mahead, mlo, mhi,
    send, recv,
):
    s = lax.axis_index("stream")
    w = lax.axis_index("wall")
    par = lax.rem(s, 2)
    partner = s + 1 - 2 * par
    first_w, last_w = w == 0, w == nw - 1
    tile = out.shape[2:]

    def rows(n, size):
        return pl.ds(pl.multiple_of(n * size, size), size)

    def copy(k, source, target, device):
        return pltpu.make_async_remote_copy(
            src_ref=source, dst_ref=target, send_sem=send.at[k], recv_sem=recv.at[k],
            device_id=device, device_id_type=MESH,
        )

    def c_mask():
        return copy(0, mrow, mahead, {"stream": s - 1})

    def c_map():
        return copy(1, ss.at[par], ss.at[par], {"stream": partner})

    def c_low(it):
        return copy(2 + 4 * it, lout.at[it], lin.at[it], {"wall": w + 1})

    def c_up(it):
        return copy(3 + 4 * it, uout.at[it], uin.at[it], {"wall": w - 1})

    def c_off(it):
        return copy(4 + 4 * it, oo.at[it, par], oo.at[it, par], {"stream": partner})

    def c_chain(it):
        return copy(5 + 4 * it, cout.at[it], cin.at[it], {"stream": s - 2})

    base = 2 + 4 * ITERS

    def c_halo_up(it):
        return copy(base + 2 * it, hhi_out.at[it], hlo.at[it], {"wall": w + 1})

    def c_halo_down(it):
        return copy(base + 1 + 2 * it, hlo_out.at[it], hhi.at[it], {"wall": w - 1})

    barrier = pltpu.get_barrier_semaphore()
    peers = [
        (w > 0, {"wall": w - 1}),
        (w < nw - 1, {"wall": w + 1}),
        (s >= 1, {"stream": s - 1}),
        (s < ns - 1, {"stream": s + 1}),
        (s >= 2, {"stream": s - 2}),
        (s < ns - 2, {"stream": s + 2}),
    ]
    count = 0
    for there, device in peers:
        count = count + jnp.where(there, 1, 0)

        @pl.when(there)
        def _(device=device):
            pl.semaphore_signal(barrier, inc=1, device_id=device, device_id_type=MESH)

    pl.semaphore_wait(barrier, count)

    sub = lax.broadcasted_iota(jnp.int32, tile, 0)
    lo = jnp.zeros(tile, jnp.int32)
    hi = jnp.zeros(tile, jnp.int32)
    for j in range(CJ):
        lo = jnp.where(sub == j, off[0, j], lo)
        hi = jnp.where(sub == j, off[0, j] + cnt[0, j], hi)
    mlo[...] = lo
    mhi[...] = hi
    mrow[...] = jnp.where((lo <= 0) & (hi > 0), 1.0, 0.0)

    @pl.when(s > 0)
    def _():
        c_mask().start()

    @pl.when(s == ns - 1)
    def _():
        mahead[...] = jnp.zeros(tile, jnp.float32)

    def active(i):
        return (mlo[...] <= i) & (mhi[...] > i)

    def transposed(target, source, number):
        @pl.loop(0, number)
        def _(n):
            for i in range(CI):
                target[n, pl.ds(i, CJ, stride=CI), :] = source[n, i].astype(jnp.float32)

    @pl.loop(0, NF * NF)
    def _(n):
        for i in range(CI):
            sif[n, i * CJ:(i + 1) * CJ, :] = si[n, i].astype(jnp.float32)

    @pl.loop(0, NF)
    def _(n):
        for i in range(CI):
            flf[n, i * CJ:(i + 1) * CJ, :] = fl[n, i].astype(jnp.float32)
            rlo[n, i:i + 1, :] = rem[n, i].astype(jnp.float32)[:1]
            rhi[n, i:i + 1, :] = rem[NF + n, i].astype(jnp.float32)[CJ - 1:]

    @pl.loop(0, NF)
    def _(c):
        start = tuple(
            jnp.full(tile, jnp.where(c == f, 1.0, 0.0), jnp.float32) for f in range(NF)
        )

        def step(t, state):
            i = CI - 1 - t
            r = rows(i, CJ)
            v = [flf[f, r, :] * state[f] for f in range(NF)]
            on = active(i)
            return tuple(
                jnp.where(on, tree_sum([sif[f * NF + e, r, :] * v[f] for f in range(NF)]), state[e])
                for e in range(NF)
            )

        final = lax.fori_loop(0, CI, step, start)
        for e in range(NF):
            ss[par, e * NF + c] = final[e]

    c_map().start()

    transposed(pt, wp, NF * NF)
    transposed(low, wl, NF)
    transposed(up, wu, NF)
    transposed(rhs, src, NF)

    zero = tuple(jnp.zeros(tile, jnp.float32) for _ in range(NF))

    def lower(it):
        @pl.when(first_w)
        def _():
            lin[it] = jnp.zeros((NF,) + tile, jnp.float32)

        @pl.when(w > 0)
        def _():
            c_low(it).wait_recv()

        def step(j, state):
            r = rows(j, CI)
            v = [rhs[f, r, :] + low[f, r, :] * state[f] for f in range(NF)]
            new = tuple(
                tree_sum([pt[e * NF + f, r, :] * v[f] for f in range(NF)]) for e in range(NF)
            )
            for e in range(NF):
                lpt[e, r, :] = new[e]
            return new

        final = lax.fori_loop(0, CJ, step, tuple(lin[it, f] for f in range(NF)))
        for f in range(NF):
            lout[it, f] = final[f]

        @pl.when(w < nw - 1)
        def _():
            c_low(it).start()

    def upper(it):
        @pl.when(last_w)
        def _():
            uin[it] = jnp.zeros((NF,) + tile, jnp.float32)

        @pl.when(w < nw - 1)
        def _():
            c_up(it).wait_recv()

        def step(t, state):
            j = CJ - 1 - t
            r = rows(j, CI)
            v = [up[f, r, :] * state[f] for f in range(NF)]
            new = tuple(
                lpt[e, r, :] + tree_sum([pt[e * NF + f, r, :] * v[f] for f in range(NF)])
                for e in range(NF)
            )
            for e in range(NF):
                upn[e, pl.ds(j, CI, stride=CJ), :] = new[e]
            return new

        final = lax.fori_loop(0, CJ, step, tuple(uin[it, f] for f in range(NF)))
        for f in range(NF):
            uout[it, f] = final[f]

        @pl.when(w > 0)
        def _():
            c_up(it).start()

    def sweep(start, emit):
        def step(t, state):
            i = CI - 1 - t
            r = rows(i, CJ)
            v = [upn[f, r, :] + flf[f, r, :] * state[f] for f in range(NF)]
            on = active(i)
            new = tuple(
                jnp.where(on, tree_sum([sif[f * NF + e, r, :] * v[f] for f in range(NF)]), state[e])
                for e in range(NF)
            )
            if emit is not None:
                emit(i, [jnp.where(on, part, 0.0) for part in new])
            return new

        return lax.fori_loop(0, CI, step, start)

    def through(which, it, state):
        return [
            oo[it, which, e] + tree_sum([ss[which, e * NF + f] * state[f] for f in range(NF)])
            for e in range(NF)
        ]

    def stream(it, emit):
        final = sweep(zero, None)
        for f in range(NF):
            oo[it, par, f] = final[f]
        c_off(it).start()

        @pl.when(s >= ns - 2)
        def _():
            cin[it] = jnp.zeros((NF,) + tile, jnp.float32)

        if it == 0:
            c_map().wait_recv()
        c_off(it).wait_recv()

        @pl.when(s < ns - 2)
        def _():
            c_chain(it).wait_recv()

        entering = [cin[it, f] for f in range(NF)]
        middle = through(1, it, entering)
        leaving = through(0, it, middle)
        for f in range(NF):
            cout[it, f] = leaving[f]

        @pl.when(s >= 2)
        def _():
            c_chain(it).start()

        mine = tuple(jnp.where(par == 1, entering[f], middle[f]) for f in range(NF))
        sweep(mine, emit)
        return mine

    for it in range(ITERS):
        lower(it)
        upper(it)
        if it == ITERS - 1:
            def emit(i, values):
                for f in range(NF):
                    out[f, i] = values[f]

            stream(it, emit)
            continue

        def emit(i, values):
            for f in range(NF):
                psi[f, i] = values[f]
                hlo_out[it, f, pl.ds(i, 1), :] = values[f][:1]
                hhi_out[it, f, pl.ds(i, 1), :] = values[f][CJ - 1:]

        mine = stream(it, emit)

        @pl.when(w < nw - 1)
        def _(it=it):
            c_halo_up(it).start()

        @pl.when(w > 0)
        def _(it=it):
            c_halo_down(it).start()

        if it == 0:
            @pl.when(s < ns - 1)
            def _():
                c_mask().wait_recv()

        for f in range(NF):
            psi[f, CI] = mahead[...] * mine[f]

        @pl.loop(0, CI)
        def _(i):
            for f in range(NF):
                here = psi[f, i]
                below = jnp.where(sub == 0, 0.0, pltpu.roll(here, 1, 0))
                above = jnp.where(sub == CJ - 1, 0.0, pltpu.roll(here, CJ - 1, 0))
                total = rem[f, i].astype(jnp.float32) * below
                total = total + rem[NF + f, i].astype(jnp.float32) * above
                total = total + rem[2 * NF + f, i].astype(jnp.float32) * psi[f, i + 1]
                rhs[f, pl.ds(i, CJ, stride=CI), :] = src[f, i] + total

        @pl.when(w > 0)
        def _(it=it):
            c_halo_up(it).wait_recv()
            for f in range(NF):
                rhs[f, :CI, :] += rlo[f] * hlo[it, f]

        @pl.when(w < nw - 1)
        def _(it=it):
            c_halo_down(it).wait_recv()
            for f in range(NF):
                rhs[f, (CJ - 1) * CI:, :] += rhi[f] * hhi[it, f]

    c_map().wait_send()

    @pl.when(s > 0)
    def _():
        c_mask().wait_send()

    for it in range(ITERS):
        c_off(it).wait_send()

        @pl.when(s >= 2)
        def _(it=it):
            c_chain(it).wait_send()

        @pl.when(w < nw - 1)
        def _(it=it):
            c_low(it).wait_send()
            if it < ITERS - 1:
                c_halo_up(it).wait_send()

        @pl.when(w > 0)
        def _(it=it):
            c_up(it).wait_send()
            if it < ITERS - 1:
                c_halo_down(it).wait_send()


def solution(mesh):
    ns, nw = mesh.shape["stream"], mesh.shape["wall"]

    def local(src, wp, wl, wu, si, fl, rem, cnt, off):
        NF, CI, CJ, CK = src.shape
        f32 = jnp.float32

        def buf(*lead):
            return pltpu.VMEM(lead + (CK,), f32)

        state = (NF, CI)
        plane = (NF, CJ)
        copies = 2 + 6 * ITERS
        vmem = pl.BlockSpec(memory_space=pltpu.VMEM)
        smem = pl.BlockSpec(memory_space=pltpu.SMEM)
        return pl.pallas_call(
            functools.partial(kernel, ns, nw, NF, CI, CJ),
            out_shape=jax.ShapeDtypeStruct(src.shape, f32),
            in_specs=[vmem] * 7 + [smem] * 2,
            out_specs=vmem,
            scratch_shapes=[
                buf(NF * NF, CI * CJ),
                buf(NF, CI * CJ),
                buf(NF, CI * CJ),
                buf(NF, CI * CJ),
                buf(NF, CI * CJ),
                buf(NF, CI * CJ),
                buf(NF * NF, CI * CJ),
                buf(NF, CI * CJ),
                buf(2, NF * NF, CJ),
                buf(ITERS, 2, *plane),
                buf(ITERS, *plane),
                buf(ITERS, *plane),
                buf(ITERS, *state),
                buf(ITERS, *state),
                buf(ITERS, *state),
                buf(ITERS, *state),
                buf(ITERS, *state),
                buf(ITERS, *state),
                buf(ITERS, *state),
                buf(ITERS, *state),
                buf(*state),
                buf(*state),
                buf(NF, CI + 1, CJ),
                buf(CJ),
                buf(CJ),
                pltpu.VMEM((CJ, CK), jnp.int32),
                pltpu.VMEM((CJ, CK), jnp.int32),
                pltpu.SemaphoreType.DMA((copies,)),
                pltpu.SemaphoreType.DMA((copies,)),
            ],
            compiler_params=pltpu.CompilerParams(
                collective_id=0, has_side_effects=True, vmem_limit_bytes=56 << 20
            ),
        )(
            src,
            wp.reshape((NF * NF,) + wp.shape[2:]),
            wl,
            wu,
            si.reshape((NF * NF,) + si.shape[2:]),
            fl,
            rem.reshape((3 * NF,) + rem.shape[2:]),
            cnt,
            off,
        )

    cell = P(None, "stream", "wall", None)
    block = P(None, None, "stream", "wall", None)
    flat = P("stream", "wall")
    return jax.shard_map(
        local,
        mesh=mesh,
        in_specs=(cell, block, cell, cell, block, cell, block, flat, flat),
        out_specs=cell,
        check_vma=False,
    )
```

```python
import functools

import jax
import jax.numpy as jnp
from jax import lax
from jax.experimental import pallas as pl
from jax.experimental.pallas import tpu as pltpu
from jax.sharding import PartitionSpec as P

MESH = pl.DeviceIdType.MESH
ITERS = 2
UNROLL = 4


def tree_sum(terms):
    while len(terms) > 1:
        paired = [terms[k] + terms[k + 1] for k in range(0, len(terms) - 1, 2)]
        if len(terms) % 2:
            paired.append(terms[-1])
        terms = paired
    return terms[0]


def kernel(
    ns, nw, NF, CI, CJ,
    src, wp, wl, wu, si, fl, rem, cnt, off,
    out,
    pt, rhs, low, up, lpt, upn, sif, flf,
    ss, oo, cin, cout, lin, lout, uin, uout,
    hlo_out, hhi_out, hlo, hhi, rlo, rhi, psi, mrow, mahead, mlo, mhi,
    send, recv,
):
    s = lax.axis_index("stream")
    w = lax.axis_index("wall")
    par = lax.rem(s, 2)
    partner = s + 1 - 2 * par
    first_w, last_w = w == 0, w == nw - 1
    tile = out.shape[2:]

    def rows(n, size):
        return pl.ds(pl.multiple_of(n * size, size), size)

    def copy(k, source, target, device):
        return pltpu.make_async_remote_copy(
            src_ref=source, dst_ref=target, send_sem=send.at[k], recv_sem=recv.at[k],
            device_id=device, device_id_type=MESH,
        )

    def c_mask():
        return copy(0, mrow, mahead, {"stream": s - 1})

    def c_map():
        return copy(1, ss.at[par], ss.at[par], {"stream": partner})

    def c_low(it):
        return copy(2 + 6 * it, lout.at[it], lin.at[it], {"wall": w + 1})

    def c_up(it):
        return copy(3 + 6 * it, uout.at[it], uin.at[it], {"wall": w - 1})

    def c_off(it, h):
        mine = oo.at[it, par, h]
        return copy(4 + 6 * it + h, mine, mine, {"stream": partner})

    def c_chain(it, h):
        return copy(6 + 6 * it + h, cout.at[it, h], cin.at[it, h], {"stream": s - 2})

    base = 2 + 6 * ITERS
    half = CJ // 2

    def c_halo_up(it):
        return copy(base + 2 * it, hhi_out.at[it], hlo.at[it], {"wall": w + 1})

    def c_halo_down(it):
        return copy(base + 1 + 2 * it, hlo_out.at[it], hhi.at[it], {"wall": w - 1})

    barrier = pltpu.get_barrier_semaphore()
    peers = [
        (w > 0, {"wall": w - 1}),
        (w < nw - 1, {"wall": w + 1}),
        (s >= 1, {"stream": s - 1}),
        (s < ns - 1, {"stream": s + 1}),
        (s >= 2, {"stream": s - 2}),
        (s < ns - 2, {"stream": s + 2}),
    ]
    count = 0
    for there, device in peers:
        count = count + jnp.where(there, 1, 0)

        @pl.when(there)
        def _(device=device):
            pl.semaphore_signal(barrier, inc=1, device_id=device, device_id_type=MESH)

    pl.semaphore_wait(barrier, count)

    sub = lax.broadcasted_iota(jnp.int32, tile, 0)
    lo = jnp.zeros(tile, jnp.int32)
    hi = jnp.zeros(tile, jnp.int32)
    for j in range(CJ):
        lo = jnp.where(sub == j, off[0, j], lo)
        hi = jnp.where(sub == j, off[0, j] + cnt[0, j], hi)
    mlo[...] = lo
    mhi[...] = hi
    mrow[...] = jnp.where((lo <= 0) & (hi > 0), 1.0, 0.0)

    @pl.when(s > 0)
    def _():
        c_mask().start()

    @pl.when(s == ns - 1)
    def _():
        mahead[...] = jnp.zeros(tile, jnp.float32)

    def active(i):
        return (mlo[...] <= i) & (mhi[...] > i)

    def transposed(target, source, number):
        @pl.loop(0, number)
        def _(n):
            for i in range(CI):
                target[n, pl.ds(i, CJ, stride=CI), :] = source[n, i].astype(jnp.float32)

    transposed(pt, wp, NF * NF)
    transposed(low, wl, NF)
    transposed(rhs, src, NF)

    zero = tuple(jnp.zeros(tile, jnp.float32) for _ in range(NF))

    def prepare():
        @pl.loop(0, NF * NF)
        def _(n):
            for i in range(CI):
                sif[n, i * CJ:(i + 1) * CJ, :] = si[n, i].astype(jnp.float32)

        @pl.loop(0, NF)
        def _(n):
            for i in range(CI):
                flf[n, i * CJ:(i + 1) * CJ, :] = fl[n, i].astype(jnp.float32)
                rlo[n, i:i + 1, :] = rem[n, i].astype(jnp.float32)[:1]
                rhi[n, i:i + 1, :] = rem[NF + n, i].astype(jnp.float32)[CJ - 1:]

        @pl.loop(0, NF)
        def _(c):
            start = tuple(
                jnp.full(tile, jnp.where(c == f, 1.0, 0.0), jnp.float32) for f in range(NF)
            )

            def step(t, state):
                i = CI - 1 - t
                r = rows(i, CJ)
                v = [flf[f, r, :] * state[f] for f in range(NF)]
                on = active(i)
                return tuple(
                    jnp.where(on, tree_sum([sif[f * NF + e, r, :] * v[f] for f in range(NF)]), state[e])
                    for e in range(NF)
                )

            final = lax.fori_loop(0, CI, step, start, unroll=UNROLL)
            for e in range(NF):
                ss[par, e * NF + c] = final[e]

        c_map().start()
        transposed(up, wu, NF)

    def lower(it):
        @pl.when(first_w)
        def _():
            lin[it] = jnp.zeros((NF,) + tile, jnp.float32)

        @pl.when(w > 0)
        def _():
            c_low(it).wait_recv()

        def step(j, state):
            r = rows(j, CI)
            v = [rhs[f, r, :] + low[f, r, :] * state[f] for f in range(NF)]
            new = tuple(
                tree_sum([pt[e * NF + f, r, :] * v[f] for f in range(NF)]) for e in range(NF)
            )
            for e in range(NF):
                lpt[e, r, :] = new[e]
            return new

        final = lax.fori_loop(0, CJ, step, tuple(lin[it, f] for f in range(NF)), unroll=UNROLL)
        for f in range(NF):
            lout[it, f] = final[f]

        @pl.when(w < nw - 1)
        def _():
            c_low(it).start()

    def upper(it):
        @pl.when(last_w)
        def _():
            uin[it] = jnp.zeros((NF,) + tile, jnp.float32)

        @pl.when(w < nw - 1)
        def _():
            c_up(it).wait_recv()

        def step(t, state):
            j = CJ - 1 - t
            r = rows(j, CI)
            v = [up[f, r, :] * state[f] for f in range(NF)]
            new = tuple(
                lpt[e, r, :] + tree_sum([pt[e * NF + f, r, :] * v[f] for f in range(NF)])
                for e in range(NF)
            )
            for e in range(NF):
                upn[e, pl.ds(j, CI, stride=CJ), :] = new[e]
            return new

        final = lax.fori_loop(0, CJ, step, tuple(uin[it, f] for f in range(NF)), unroll=UNROLL)
        for f in range(NF):
            uout[it, f] = final[f]

        @pl.when(w > 0)
        def _():
            c_up(it).start()

    def sweep(start, emit):
        def step(t, state):
            i = CI - 1 - t
            r = rows(i, CJ)
            v = [upn[f, r, :] + flf[f, r, :] * state[f] for f in range(NF)]
            on = active(i)
            new = tuple(
                jnp.where(on, tree_sum([sif[f * NF + e, r, :] * v[f] for f in range(NF)]), state[e])
                for e in range(NF)
            )
            if emit is not None:
                emit(i, [jnp.where(on, part, 0.0) for part in new])
            return new

        return lax.fori_loop(0, CI, step, start, unroll=UNROLL)

    def through(which, it, h, state):
        part = pl.ds(h * half, half)
        return [
            oo[it, which, h, e]
            + tree_sum([ss[which, e * NF + f, part, :] * state[f] for f in range(NF)])
            for e in range(NF)
        ]

    def stream(it, emit):
        final = sweep(zero, None)
        for h in range(2):
            for f in range(NF):
                oo[it, par, h, f] = final[f][h * half:(h + 1) * half]
            c_off(it, h).start()

        @pl.when(s >= ns - 2)
        def _():
            cin[it] = jnp.zeros((2, NF, half) + tile[1:], jnp.float32)

        if it == 0:
            c_map().wait_recv()
        parts = []
        for h in range(2):
            c_off(it, h).wait_recv()

            @pl.when(s < ns - 2)
            def _(h=h):
                c_chain(it, h).wait_recv()

            entering = [cin[it, h, f] for f in range(NF)]
            middle = through(1, it, h, entering)
            leaving = through(0, it, h, middle)
            for f in range(NF):
                cout[it, h, f] = leaving[f]

            @pl.when(s >= 2)
            def _(h=h):
                c_chain(it, h).start()

            parts.append([jnp.where(par == 1, entering[f], middle[f]) for f in range(NF)])

        mine = tuple(jnp.concatenate([parts[0][f], parts[1][f]], axis=0) for f in range(NF))
        sweep(mine, emit)
        return mine

    for it in range(ITERS):
        if it == 0:
            pl.when(w < nw // 2)(lambda: lower(0))
            prepare()
            pl.when(w >= nw // 2)(lambda: lower(0))
        else:
            lower(it)
        upper(it)
        if it == ITERS - 1:
            def emit(i, values):
                for f in range(NF):
                    out[f, i] = values[f]

            stream(it, emit)
            continue

        def emit(i, values):
            for f in range(NF):
                psi[f, i] = values[f]
                hlo_out[it, f, pl.ds(i, 1), :] = values[f][:1]
                hhi_out[it, f, pl.ds(i, 1), :] = values[f][CJ - 1:]

        mine = stream(it, emit)

        @pl.when(w < nw - 1)
        def _(it=it):
            c_halo_up(it).start()

        @pl.when(w > 0)
        def _(it=it):
            c_halo_down(it).start()

        if it == 0:
            @pl.when(s < ns - 1)
            def _():
                c_mask().wait_recv()

        for f in range(NF):
            psi[f, CI] = mahead[...] * mine[f]

        @pl.loop(0, CI)
        def _(i):
            for f in range(NF):
                here = psi[f, i]
                below = jnp.where(sub == 0, 0.0, pltpu.roll(here, 1, 0))
                above = jnp.where(sub == CJ - 1, 0.0, pltpu.roll(here, CJ - 1, 0))
                total = rem[f, i].astype(jnp.float32) * below
                total = total + rem[NF + f, i].astype(jnp.float32) * above
                total = total + rem[2 * NF + f, i].astype(jnp.float32) * psi[f, i + 1]
                rhs[f, pl.ds(i, CJ, stride=CI), :] = src[f, i] + total

        @pl.when(w > 0)
        def _(it=it):
            c_halo_up(it).wait_recv()
            for f in range(NF):
                rhs[f, :CI, :] += rlo[f] * hlo[it, f]

        @pl.when(w < nw - 1)
        def _(it=it):
            c_halo_down(it).wait_recv()
            for f in range(NF):
                rhs[f, (CJ - 1) * CI:, :] += rhi[f] * hhi[it, f]

    c_map().wait_send()

    @pl.when(s > 0)
    def _():
        c_mask().wait_send()

    for it in range(ITERS):
        for h in range(2):
            c_off(it, h).wait_send()

        @pl.when(s >= 2)
        def _(it=it):
            for h in range(2):
                c_chain(it, h).wait_send()

        @pl.when(w < nw - 1)
        def _(it=it):
            c_low(it).wait_send()
            if it < ITERS - 1:
                c_halo_up(it).wait_send()

        @pl.when(w > 0)
        def _(it=it):
            c_up(it).wait_send()
            if it < ITERS - 1:
                c_halo_down(it).wait_send()


def solution(mesh):
    ns, nw = mesh.shape["stream"], mesh.shape["wall"]

    def local(src, wp, wl, wu, si, fl, rem, cnt, off):
        NF, CI, CJ, CK = src.shape
        f32 = jnp.float32

        def buf(*lead):
            return pltpu.VMEM(lead + (CK,), f32)

        state = (NF, CI)
        copies = 2 + 8 * ITERS
        vmem = pl.BlockSpec(memory_space=pltpu.VMEM)
        smem = pl.BlockSpec(memory_space=pltpu.SMEM)
        return pl.pallas_call(
            functools.partial(kernel, ns, nw, NF, CI, CJ),
            out_shape=jax.ShapeDtypeStruct(src.shape, f32),
            in_specs=[vmem] * 7 + [smem] * 2,
            out_specs=vmem,
            scratch_shapes=[
                buf(NF * NF, CI * CJ),
                buf(NF, CI * CJ),
                buf(NF, CI * CJ),
                buf(NF, CI * CJ),
                buf(NF, CI * CJ),
                buf(NF, CI * CJ),
                buf(NF * NF, CI * CJ),
                buf(NF, CI * CJ),
                buf(2, NF * NF, CJ),
                buf(ITERS, 2, 2, NF, CJ // 2),
                buf(ITERS, 2, NF, CJ // 2),
                buf(ITERS, 2, NF, CJ // 2),
                buf(ITERS, *state),
                buf(ITERS, *state),
                buf(ITERS, *state),
                buf(ITERS, *state),
                buf(ITERS, *state),
                buf(ITERS, *state),
                buf(ITERS, *state),
                buf(ITERS, *state),
                buf(*state),
                buf(*state),
                buf(NF, CI + 1, CJ),
                buf(CJ),
                buf(CJ),
                pltpu.VMEM((CJ, CK), jnp.int32),
                pltpu.VMEM((CJ, CK), jnp.int32),
                pltpu.SemaphoreType.DMA((copies,)),
                pltpu.SemaphoreType.DMA((copies,)),
            ],
            compiler_params=pltpu.CompilerParams(
                collective_id=0, has_side_effects=True, vmem_limit_bytes=32 << 20
            ),
        )(
            src,
            wp.reshape((NF * NF,) + wp.shape[2:]),
            wl,
            wu,
            si.reshape((NF * NF,) + si.shape[2:]),
            fl,
            rem.reshape((3 * NF,) + rem.shape[2:]),
            cnt,
            off,
        )

    cell = P(None, "stream", "wall", None)
    block = P(None, None, "stream", "wall", None)
    flat = P("stream", "wall")
    return jax.shard_map(
        local,
        mesh=mesh,
        in_specs=(cell, block, cell, cell, block, cell, block, flat, flat),
        out_specs=cell,
        check_vma=False,
    )
```
